768 devices in a mesh: outer: 96 (over z, x, core), inner: 8 (over y).
Axes of the slice: x: 4, y: 8, z: 12, core: 2. Of those that a mesh axis runs over, the one named last changes fastest.
Arguments:
- query_rows: bfloat16 [196608, 256], P(('outer', 'inner')), may hold values from -6 to 6
- key_rows: bfloat16 [196608, 256], P(('outer', 'inner')), may hold values from -6 to 6
- value_rows: bfloat16 [196608, 256], P(('outer', 'inner')), may hold values from -6 to 6
- grad_output: bfloat16 [196608, 256], P(('outer', 'inner')), may hold values from -6 to 6
Outputs:
- attended: bfloat16 [196608, 256], P(('outer', 'inner'))
- grad_queries: bfloat16 [196608, 256], P(('outer', 'inner'))
- grad_keys: bfloat16 [196608, 256], P(('outer', 'inner'))
- grad_values: bfloat16 [196608, 256], P(('outer', 'inner'))
The draws below stay inside these ranges and needn't reach their ends.
All inputs are finite; a program needn't handle non-finite values.
Results may differ from the reference program's by a relative error of at most 0.014.
Values may be sent and summed in bfloat16 or wider, within the bound.
A program may use at most 32 MiB of HBM per device.

```python
import jax
import jax.numpy as jnp
from jax import lax

H = 2
DH = 128
TOK_DEV = 256
TOKENS = 196608


def levels(stream_key, shape, split, smallest, largest):
    loudness, own = 1.0, jax.random.fold_in(stream_key, 6)
    for dim, parts in split:
        draws = jnp.exp(jax.random.uniform(jax.random.fold_in(own, dim), (parts,), jnp.float32, smallest / len(split), largest / len(split)))
        loudness = loudness * jnp.repeat(draws, shape[dim] // parts).reshape([-1 if axis == dim else 1 for axis in range(len(shape))])
    return loudness


def scatter_about(rng, dims, spread, reach, pieces=(), kind=jnp.bfloat16):
    entries = spread * jax.random.normal(rng, dims, jnp.float32)
    if pieces:
        entries = entries * levels(rng, dims, pieces, -0.22, 0.18)
    return jnp.clip(entries, -reach, reach).astype(kind)


def setup_inputs(seed: int = 0) -> dict:
    keys = jax.random.split(jax.random.key(seed), 5)
    query_rows = scatter_about(keys[0], (TOKENS, H * DH), 1.0, 6.0, ((0, 768),))
    key_rows = scatter_about(keys[1], (TOKENS, H * DH), 1.0, 6.0, ((0, 768),))
    value_rows = scatter_about(keys[2], (TOKENS, H * DH), 1.0, 6.0, ((0, 768),))
    grad_output = scatter_about(keys[3], (TOKENS, H * DH), 1.0, 6.0, ((0, 768),))
    return {"query_rows": query_rows, "key_rows": key_rows, "value_rows": value_rows, "grad_output": grad_output}


eps = 1e-06

def causal_scores(left, right, rows):
    lower = jnp.tril(jnp.ones((rows, rows), dtype=bool))
    raw = jnp.einsum('thd,shd->hts', left, right)
    return jnp.where(lower[None], raw, 0.0).astype(jnp.bfloat16)

def reference(query_rows, key_rows, value_rows, grad_output):
    rows = TOK_DEV
    shaped = [x.reshape(-1, rows, H, DH) for x in (query_rows, key_rows, value_rows, grad_output)]

    def forward_step(prefix, blocks):
        query, key_blk, value, grad_out = blocks
        q_f = query.astype(jnp.float32)
        k_f = key_blk.astype(jnp.float32)
        v_f = value.astype(jnp.float32)
        piece = jnp.einsum('thd,the->hde', k_f, v_f).astype(jnp.bfloat16)
        scores = causal_scores(q_f, k_f, rows).astype(jnp.float32)
        prefix_round = prefix.astype(jnp.bfloat16).astype(jnp.float32)
        mixed = jnp.einsum('hts,she->the', scores, v_f) + jnp.einsum('thd,hde->the', q_f, prefix_round)
        inverse = lax.rsqrt(lax.optimization_barrier(jnp.mean(mixed * mixed, axis=-1, keepdims=True)) + eps)
        normed = mixed * inverse
        attended = normed.astype(jnp.bfloat16)
        g_f = grad_out.astype(jnp.float32)
        grad_mixed = (inverse * (g_f - normed * lax.optimization_barrier(jnp.mean(g_f * normed, axis=-1, keepdims=True)))).astype(jnp.bfloat16)
        gm_f = grad_mixed.astype(jnp.float32)
        grad_scores = causal_scores(gm_f, v_f, rows).astype(jnp.float32)
        grad_q = jnp.einsum('hts,shd->thd', grad_scores, k_f) + jnp.einsum('the,hde->thd', gm_f, prefix_round)
        return (prefix + piece.astype(jnp.float32), (attended, grad_q.astype(jnp.bfloat16), grad_mixed))
    start = jnp.zeros((H, DH, DH), jnp.float32)
    _, (attended, grad_q, grad_mixed) = lax.scan(forward_step, start, tuple(shaped))

    def backward_step(suffix, blocks):
        query, key_blk, value, grad_m = blocks
        q_f = query.astype(jnp.float32)
        k_f = key_blk.astype(jnp.float32)
        v_f = value.astype(jnp.float32)
        gm_f = grad_m.astype(jnp.float32)
        back_piece = jnp.einsum('thd,the->hde', q_f, gm_f).astype(jnp.bfloat16)
        suffix_round = suffix.astype(jnp.bfloat16).astype(jnp.float32)
        scores = causal_scores(q_f, k_f, rows).astype(jnp.float32)
        grad_scores = causal_scores(gm_f, v_f, rows).astype(jnp.float32)
        grad_k = jnp.einsum('hts,thd->shd', grad_scores, q_f) + jnp.einsum('she,hde->shd', v_f, suffix_round)
        grad_v = jnp.einsum('hts,the->she', scores, gm_f) + jnp.einsum('shd,hde->she', k_f, suffix_round)
        return (suffix + back_piece.astype(jnp.float32), (grad_k.astype(jnp.bfloat16), grad_v.astype(jnp.bfloat16)))
    _, (grad_k, grad_v) = lax.scan(backward_step, start, (shaped[0], shaped[1], shaped[2], grad_mixed), reverse=True)
    width = H * DH
    return (attended.reshape(-1, width), grad_q.reshape(-1, width), grad_k.reshape(-1, width), grad_v.reshape(-1, width))
```

```python
import functools

import jax
import jax.numpy as jnp
from jax import lax
from jax.experimental import pallas as pl
from jax.experimental.pallas import tpu as pltpu
from jax.sharding import PartitionSpec as P

H = 2
DH = 128
X = 4
C = 2
eps = 1e-06
MESH = pl.DeviceIdType.MESH
F32 = jnp.float32
BF16 = jnp.bfloat16


def mm(a, b):
    return lax.dot_general(a, b, (((1,), (0,)), ((), ())), preferred_element_type=F32)


def mm_nt(a, b):
    return lax.dot_general(a, b, (((1,), (1,)), ((), ())), preferred_element_type=F32)


def mm_tn(a, b):
    return lax.dot_general(a, b, (((0,), (0,)), ((), ())), preferred_element_type=F32)


def kernel(
    Z,
    Y,
    q_ref,
    k_ref,
    v_ref,
    g_ref,
    att_ref,
    gq_ref,
    gk_ref,
    gv_ref,
    piece,
    inbox,
    xbox,
    zbox,
    outbox,
    state,
    scores,
    mix,
    acc_k,
    acc_v,
    a_sem,
    x_sem,
    r_sem,
    z_send,
    z_recv,
):
    J = C * Y
    rows = (H * DH) // J
    tokens = q_ref.shape[0]
    outer = lax.axis_index("outer")
    y = lax.axis_index("inner")
    c = lax.rem(outer, C)
    x = lax.rem(outer // C, X)
    z = outer // (C * X)
    me = c * Y + y

    def device(zz, xx, cc, yy):
        return ((zz * X + xx) * C + cc, yy)

    def far_first(n):
        return sorted(range(1, n), key=lambda d: -min(d, n - d))

    peers = []
    for d in far_first(Y) + [0]:
        for e in range(C):
            if d or e:
                cc, yy = lax.rem(c + e, C), lax.rem(y + d, Y)
                peers.append((cc * Y + yy, device(z, x, cc, yy)))
    x_peers = [device(z, lax.rem(x + d, X), c, y) for d in far_first(X)]
    z_peers = [(lax.rem(z + d, Z), device(lax.rem(z + d, Z), x, c, y)) for d in far_first(Z)]

    barrier = pltpu.get_barrier_semaphore()
    everyone = [p for _, p in z_peers] + x_peers + [p for _, p in peers]
    for p in everyone:
        pl.semaphore_signal(barrier, inc=1, device_id=p, device_id_type=MESH)

    def part(ref, h):
        return ref[:, h * DH : (h + 1) * DH]

    def chunk(j):
        return pl.ds(pl.multiple_of(j * rows, rows), rows)

    lower = lax.broadcasted_iota(jnp.int32, (tokens, tokens), 0) >= lax.broadcasted_iota(
        jnp.int32, (tokens, tokens), 1
    )

    def spread(s):
        copies = []
        for j, p in peers:
            copy = pltpu.make_async_remote_copy(
                src_ref=piece.at[s, chunk(j)],
                dst_ref=inbox.at[s, me],
                send_sem=a_sem.at[s, 0],
                recv_sem=a_sem.at[s, 1],
                device_id=p,
                device_id_type=MESH,
            )
            copy.start()
        inbox[s, me] = piece[s, chunk(me)]

    def all_of(ref, sem):
        pltpu.make_async_copy(ref, ref, sem).wait()

    def carry(s):
        forward = s == 0
        all_of(inbox.at[s, pl.ds(0, J - 1)], a_sem.at[s, 1])
        run = jnp.zeros((rows, DH), F32)
        enter = [None] * J
        for j in range(J) if forward else reversed(range(J)):
            enter[j] = run
            run = run + inbox[s, j].astype(F32)
        xbox[s, x] = run
        for p in x_peers:
            pltpu.make_async_remote_copy(
                src_ref=xbox.at[s, x],
                dst_ref=xbox.at[s, x],
                send_sem=x_sem.at[s, 0],
                recv_sem=x_sem.at[s, 1],
                device_id=p,
                device_id_type=MESH,
            ).start()
        all_of(xbox.at[s, pl.ds(0, X - 1)], x_sem.at[s, 1])
        before = jnp.zeros((rows, DH), F32)
        total = jnp.zeros((rows, DH), F32)
        for i in range(X):
            term = xbox[s, i]
            total = total + term
            before = before + jnp.where(i < x if forward else i > x, term, 0.0)
        zbox[s, z] = total.astype(zbox.dtype)
        for zz, p in z_peers:

            @pl.when(zz > z if forward else zz < z)
            def _():
                pltpu.make_async_remote_copy(
                    src_ref=zbox.at[s, z],
                    dst_ref=zbox.at[s, z],
                    send_sem=z_send.at[s, zz],
                    recv_sem=z_recv.at[s, z],
                    device_id=p,
                    device_id_type=MESH,
                ).start()

        def take(i, sofar):
            pltpu.make_async_copy(zbox.at[s, i], zbox.at[s, i], z_recv.at[s, i]).wait()
            return sofar + zbox[s, i].astype(F32)

        before = lax.fori_loop(0 if forward else z + 1, z if forward else Z, take, before)
        for j in range(J):
            outbox[s, j] = (enter[j] + before).astype(BF16)
        for j, p in peers:
            pltpu.make_async_remote_copy(
                src_ref=outbox.at[s, j],
                dst_ref=state.at[s, chunk(me)],
                send_sem=r_sem.at[s, 0],
                recv_sem=r_sem.at[s, 1],
                device_id=p,
                device_id_type=MESH,
            ).start()
        state[s, chunk(me)] = outbox[s, me]

    def arrive(s):
        all_of(outbox.at[s, pl.ds(0, J - 1)], r_sem.at[s, 1])

    def drain(s):
        forward = s == 0
        all_of(inbox.at[s, pl.ds(0, J - 1)], a_sem.at[s, 0])
        all_of(xbox.at[s, pl.ds(0, X - 1)], x_sem.at[s, 0])
        all_of(outbox.at[s, pl.ds(0, J - 1)], r_sem.at[s, 0])

        def sent(i, _):
            pltpu.make_async_copy(zbox.at[s, z], zbox.at[s, z], z_send.at[s, i]).wait()
            return 0

        lax.fori_loop(z + 1 if forward else 0, Z if forward else z, sent, 0)

    for h in range(H):
        piece[0, h * DH : (h + 1) * DH] = mm_tn(part(k_ref, h), part(v_ref, h)).astype(BF16)
    pl.semaphore_wait(barrier, len(everyone))
    spread(0)
    for h in range(H):
        raw = mm_nt(part(q_ref, h), part(k_ref, h))
        s_h = jnp.where(lower, raw, 0.0).astype(BF16)
        scores[h] = s_h
        mix[:, h * DH : (h + 1) * DH] = mm(s_h, part(v_ref, h))
    carry(0)
    arrive(0)
    grad_mixed = []
    for h in range(H):
        pref = state[0, h * DH : (h + 1) * DH]
        q = part(q_ref, h)
        mixed = part(mix, h) + mm(q, pref)
        inverse = lax.rsqrt(jnp.mean(mixed * mixed, axis=-1, keepdims=True) + eps)
        normed = mixed * inverse
        att_ref[:, h * DH : (h + 1) * DH] = normed.astype(BF16)
        g = part(g_ref, h).astype(F32)
        gm = (inverse * (g - normed * jnp.mean(g * normed, axis=-1, keepdims=True))).astype(BF16)
        grad_mixed.append(gm)
        piece[1, h * DH : (h + 1) * DH] = mm_tn(q, gm).astype(BF16)
    spread(1)
    for h in range(H):
        gm = grad_mixed[h]
        gs = jnp.where(lower, mm_nt(gm, part(v_ref, h)), 0.0).astype(BF16)
        pref = state[0, h * DH : (h + 1) * DH]
        gq_ref[:, h * DH : (h + 1) * DH] = (mm(gs, part(k_ref, h)) + mm_nt(gm, pref)).astype(BF16)
        acc_k[:, h * DH : (h + 1) * DH] = mm_tn(gs, part(q_ref, h))
        acc_v[:, h * DH : (h + 1) * DH] = mm_tn(scores[h], gm)
    carry(1)
    arrive(1)
    for h in range(H):
        suf = state[1, h * DH : (h + 1) * DH]
        gk_ref[:, h * DH : (h + 1) * DH] = (part(acc_k, h) + mm_nt(part(v_ref, h), suf)).astype(BF16)
        gv_ref[:, h * DH : (h + 1) * DH] = (part(acc_v, h) + mm(part(k_ref, h), suf)).astype(BF16)
    drain(0)
    drain(1)


def solution(mesh):
    Z = mesh.shape["outer"] // (X * C)
    Y = mesh.shape["inner"]
    J = C * Y
    rows = (H * DH) // J
    spec = P(("outer", "inner"), None)

    def local(q, k, v, g):
        tokens, width = q.shape
        vmem = pl.BlockSpec(memory_space=pltpu.VMEM)
        return pl.pallas_call(
            functools.partial(kernel, Z, Y),
            out_shape=[jax.ShapeDtypeStruct((tokens, width), BF16)] * 4,
            in_specs=[vmem] * 4,
            out_specs=[vmem] * 4,
            scratch_shapes=[
                pltpu.VMEM((2, H * DH, DH), BF16),
                pltpu.VMEM((2, J, rows, DH), BF16),
                pltpu.VMEM((2, X, rows, DH), F32),
                pltpu.VMEM((2, Z, rows, DH), BF16),
                pltpu.VMEM((2, J, rows, DH), BF16),
                pltpu.VMEM((2, H * DH, DH), BF16),
                pltpu.VMEM((H, tokens, tokens), BF16),
                pltpu.VMEM((tokens, width), F32),
                pltpu.VMEM((tokens, width), F32),
                pltpu.VMEM((tokens, width), F32),
                pltpu.SemaphoreType.DMA((2, 2)),
                pltpu.SemaphoreType.DMA((2, 2)),
                pltpu.SemaphoreType.DMA((2, 2)),
                pltpu.SemaphoreType.DMA((2, Z)),
                pltpu.SemaphoreType.DMA((2, Z)),
            ],
            compiler_params=pltpu.CompilerParams(collective_id=0, has_side_effects=True),
        )(q, k, v, g)

    return jax.shard_map(
        local, mesh=mesh, in_specs=(spec,) * 4, out_specs=(spec,) * 4, check_vma=False
    )
```

```python
import functools

import jax
import jax.numpy as jnp
from jax import lax
from jax.experimental import pallas as pl
from jax.experimental.pallas import tpu as pltpu
from jax.sharding import PartitionSpec as P

H = 2
DH = 128
X = 4
C = 2
eps = 1e-06
MESH = pl.DeviceIdType.MESH
F32 = jnp.float32
BF16 = jnp.bfloat16


def mm(a, b):
    return lax.dot_general(a, b, (((1,), (0,)), ((), ())), preferred_element_type=F32)


def mm_nt(a, b):
    return lax.dot_general(a, b, (((1,), (1,)), ((), ())), preferred_element_type=F32)


def mm_tn(a, b):
    return lax.dot_general(a, b, (((0,), (0,)), ((), ())), preferred_element_type=F32)


def kernel(
    Z,
    Y,
    q_hbm,
    k_hbm,
    v_hbm,
    g_hbm,
    att_ref,
    gq_ref,
    gk_ref,
    gv_ref,
    q_ref,
    k_ref,
    v_ref,
    g_ref,
    piece,
    inbox,
    xbox,
    zbox,
    outbox,
    state,
    scores,
    mix,
    acc_k,
    acc_v,
    a_sem,
    x_sem,
    r_sem,
    z_send,
    z_recv,
    in_sem,
    reply,
):
    J = C * Y
    rows = (H * DH) // J
    tokens = q_ref.shape[0]
    outer = lax.axis_index("outer")
    y = lax.axis_index("inner")
    c = lax.rem(outer, C)
    x = lax.rem(outer // C, X)
    z = outer // (C * X)
    me = c * Y + y

    def device(zz, xx, cc, yy):
        return ((zz * X + xx) * C + cc, yy)

    def far_first(n):
        return sorted(range(1, n), key=lambda d: -min(d, n - d))

    peers = []
    for d in far_first(Y) + [0]:
        for e in range(C):
            if d or e:
                cc, yy = lax.rem(c + e, C), lax.rem(y + d, Y)
                peers.append((cc * Y + yy, device(z, x, cc, yy)))
    x_peers = [device(z, lax.rem(x + d, X), c, y) for d in far_first(X)]

    barrier = pltpu.get_barrier_semaphore()
    plane = [p for _, p in peers] + x_peers
    for p in plane:
        pl.semaphore_signal(barrier, inc=1, device_id=p, device_id_type=MESH)
    loads = {}
    for i, (name, src, dst) in enumerate(
        (("k", k_hbm, k_ref), ("v", v_hbm, v_ref), ("q", q_hbm, q_ref), ("g", g_hbm, g_ref))
    ):
        loads[name] = pltpu.make_async_copy(src, dst, in_sem.at[i])
        loads[name].start()

    def greet(zz, _):
        pl.semaphore_signal(barrier, inc=1, device_id=device(zz, x, c, y), device_id_type=MESH)
        return 0

    lax.fori_loop(z + 1, Z, greet, 0)

    def part(ref, h):
        return ref[:, h * DH : (h + 1) * DH]

    def chunk(j):
        return pl.ds(pl.multiple_of(j * rows, rows), rows)

    lower = lax.broadcasted_iota(jnp.int32, (tokens, tokens), 0) >= lax.broadcasted_iota(
        jnp.int32, (tokens, tokens), 1
    )

    def spread(s):
        copies = []
        for j, p in peers:
            copy = pltpu.make_async_remote_copy(
                src_ref=piece.at[s, chunk(j)],
                dst_ref=inbox.at[s, me],
                send_sem=a_sem.at[s, 0],
                recv_sem=a_sem.at[s, 1],
                device_id=p,
                device_id_type=MESH,
            )
            copy.start()
        inbox[s, me] = piece[s, chunk(me)]

    def all_of(ref, sem):
        pltpu.make_async_copy(ref, ref, sem).wait()

    def carry(s):
        forward = s == 0
        all_of(inbox.at[s, pl.ds(0, J - 1)], a_sem.at[s, 1])
        run = jnp.zeros((rows, DH), F32)
        enter = [None] * J
        for j in range(J) if forward else reversed(range(J)):
            enter[j] = run
            run = run + inbox[s, j].astype(F32)
        xbox[s, x] = run
        for p in x_peers:
            pltpu.make_async_remote_copy(
                src_ref=xbox.at[s, x],
                dst_ref=xbox.at[s, x],
                send_sem=x_sem.at[s, 0],
                recv_sem=x_sem.at[s, 1],
                device_id=p,
                device_id_type=MESH,
            ).start()
        all_of(xbox.at[s, pl.ds(0, X - 1)], x_sem.at[s, 1])
        before = jnp.zeros((rows, DH), F32)
        total = jnp.zeros((rows, DH), F32)
        for i in range(X):
            term = xbox[s, i]
            total = total + term
            before = before + jnp.where(i < x if forward else i > x, term, 0.0)
        zbox[s, z] = total.astype(zbox.dtype)

        def send_z(zz):
            pltpu.make_async_remote_copy(
                src_ref=zbox.at[s, z],
                dst_ref=zbox.at[s, z],
                send_sem=z_send.at[s, zz],
                recv_sem=z_recv.at[s, z],
                device_id=device(zz, x, c, y),
                device_id_type=MESH,
            ).start()

        if forward:

            def later(zz, _):
                pl.semaphore_wait(reply.at[zz], 1)
                send_z(zz)
                return 0

            lax.fori_loop(z + 1, Z, later, 0)
        else:

            def earlier(zz, _):
                send_z(zz)
                return 0

            lax.fori_loop(0, z, earlier, 0)

        def take(i, sofar):
            pltpu.make_async_copy(zbox.at[s, i], zbox.at[s, i], z_recv.at[s, i]).wait()
            return sofar + zbox[s, i].astype(F32)

        before = lax.fori_loop(0 if forward else z + 1, z if forward else Z, take, before)
        for j in range(J):
            outbox[s, j] = (enter[j] + before).astype(BF16)
        for j, p in peers:
            pltpu.make_async_remote_copy(
                src_ref=outbox.at[s, j],
                dst_ref=state.at[s, chunk(me)],
                send_sem=r_sem.at[s, 0],
                recv_sem=r_sem.at[s, 1],
                device_id=p,
                device_id_type=MESH,
            ).start()
        state[s, chunk(me)] = outbox[s, me]

    def arrive(s):
        all_of(outbox.at[s, pl.ds(0, J - 1)], r_sem.at[s, 1])

    def drain(s):
        forward = s == 0
        all_of(inbox.at[s, pl.ds(0, J - 1)], a_sem.at[s, 0])
        all_of(xbox.at[s, pl.ds(0, X - 1)], x_sem.at[s, 0])
        all_of(outbox.at[s, pl.ds(0, J - 1)], r_sem.at[s, 0])

        def sent(i, _):
            pltpu.make_async_copy(zbox.at[s, z], zbox.at[s, z], z_send.at[s, i]).wait()
            return 0

        lax.fori_loop(z + 1 if forward else 0, Z if forward else z, sent, 0)

    loads["k"].wait()
    loads["v"].wait()
    for h in range(H):
        piece[0, h * DH : (h + 1) * DH] = mm_tn(part(k_ref, h), part(v_ref, h)).astype(BF16)
    pl.semaphore_wait(barrier, len(plane) + z)
    spread(0)

    def answer(zz, _):
        pl.semaphore_signal(
            reply.at[z], inc=1, device_id=device(zz, x, c, y), device_id_type=MESH
        )
        return 0

    lax.fori_loop(0, z, answer, 0)
    loads["q"].wait()
    loads["g"].wait()
    for h in range(H):
        raw = mm_nt(part(q_ref, h), part(k_ref, h))
        s_h = jnp.where(lower, raw, 0.0).astype(BF16)
        scores[h] = s_h
        mix[:, h * DH : (h + 1) * DH] = mm(s_h, part(v_ref, h))
    carry(0)
    arrive(0)
    grad_mixed = []
    for h in range(H):
        pref = state[0, h * DH : (h + 1) * DH]
        q = part(q_ref, h)
        mixed = part(mix, h) + mm(q, pref)
        inverse = lax.rsqrt(jnp.mean(mixed * mixed, axis=-1, keepdims=True) + eps)
        normed = mixed * inverse
        att_ref[:, h * DH : (h + 1) * DH] = normed.astype(BF16)
        g = part(g_ref, h).astype(F32)
        gm = (inverse * (g - normed * jnp.mean(g * normed, axis=-1, keepdims=True))).astype(BF16)
        grad_mixed.append(gm)
        piece[1, h * DH : (h + 1) * DH] = mm_tn(q, gm).astype(BF16)
    spread(1)
    for h in range(H):
        gm = grad_mixed[h]
        gs = jnp.where(lower, mm_nt(gm, part(v_ref, h)), 0.0).astype(BF16)
        pref = state[0, h * DH : (h + 1) * DH]
        gq_ref[:, h * DH : (h + 1) * DH] = (mm(gs, part(k_ref, h)) + mm_nt(gm, pref)).astype(BF16)
        acc_k[:, h * DH : (h + 1) * DH] = mm_tn(gs, part(q_ref, h))
        acc_v[:, h * DH : (h + 1) * DH] = mm_tn(scores[h], gm)
    carry(1)
    arrive(1)
    for h in range(H):
        suf = state[1, h * DH : (h + 1) * DH]
        gk_ref[:, h * DH : (h + 1) * DH] = (part(acc_k, h) + mm_nt(part(v_ref, h), suf)).astype(BF16)
        gv_ref[:, h * DH : (h + 1) * DH] = (part(acc_v, h) + mm(part(k_ref, h), suf)).astype(BF16)
    drain(0)
    drain(1)


def flush(*refs):
    n = len(refs) // 2
    sem = refs[-1]
    copies = [pltpu.make_async_copy(refs[i], refs[n + i], sem.at[i]) for i in range(n)]
    for copy in copies:
        copy.start()
    for copy in copies:
        copy.wait()


def solution(mesh):
    Z = mesh.shape["outer"] // (X * C)
    Y = mesh.shape["inner"]
    J = C * Y
    rows = (H * DH) // J
    spec = P(("outer", "inner"), None)

    def local(q, k, v, g):
        tokens, width = q.shape
        vmem = pl.BlockSpec(memory_space=pltpu.VMEM)
        block = pltpu.VMEM((tokens, width), BF16)
        hbm = pl.BlockSpec(memory_space=pl.ANY)
        results = pl.pallas_call(
            functools.partial(kernel, Z, Y),
            out_shape=[block] * 4,
            in_specs=[hbm] * 4,
            out_specs=[vmem] * 4,
            scratch_shapes=[block] * 4
            + [
                pltpu.VMEM((2, H * DH, DH), BF16),
                pltpu.VMEM((2, J, rows, DH), BF16),
                pltpu.VMEM((2, X, rows, DH), F32),
                pltpu.VMEM((2, Z, rows, DH), BF16),
                pltpu.VMEM((2, J, rows, DH), BF16),
                pltpu.VMEM((2, H * DH, DH), BF16),
                pltpu.VMEM((H, tokens, tokens), BF16),
                pltpu.VMEM((tokens, width), F32),
                pltpu.VMEM((tokens, width), F32),
                pltpu.VMEM((tokens, width), F32),
                pltpu.SemaphoreType.DMA((2, 2)),
                pltpu.SemaphoreType.DMA((2, 2)),
                pltpu.SemaphoreType.DMA((2, 2)),
                pltpu.SemaphoreType.DMA((2, Z)),
                pltpu.SemaphoreType.DMA((2, Z)),
                pltpu.SemaphoreType.DMA((4,)),
                pltpu.SemaphoreType.REGULAR((Z,)),
            ],
            compiler_params=pltpu.CompilerParams(collective_id=0, has_side_effects=True),
        )(q, k, v, g)
        return pl.pallas_call(
            flush,
            out_shape=[jax.ShapeDtypeStruct((tokens, width), BF16)] * 4,
            in_specs=[vmem] * 4,
            out_specs=[hbm] * 4,
            scratch_shapes=[pltpu.SemaphoreType.DMA((4,))],
        )(*[pltpu.with_memory_space_constraint(r, pltpu.VMEM) for r in results])

    return jax.shard_map(
        local, mesh=mesh, in_specs=(spec,) * 4, out_specs=(spec,) * 4, check_vma=False
    )
```

```python
import functools

import jax
import jax.numpy as jnp
from jax import lax
from jax.experimental import pallas as pl
from jax.experimental.pallas import tpu as pltpu
from jax.sharding import PartitionSpec as P

H = 2
DH = 128
X = 4
C = 2
eps = 1e-06
MESH = pl.DeviceIdType.MESH
F32 = jnp.float32
BF16 = jnp.bfloat16


def mm(a, b):
    return lax.dot_general(a, b, (((1,), (0,)), ((), ())), preferred_element_type=F32)


def mm_nt(a, b):
    return lax.dot_general(a, b, (((1,), (1,)), ((), ())), preferred_element_type=F32)


def mm_tn(a, b):
    return lax.dot_general(a, b, (((0,), (0,)), ((), ())), preferred_element_type=F32)


def kernel(
    Z,
    Y,
    q_hbm,
    k_hbm,
    v_hbm,
    g_hbm,
    att_ref,
    gq_ref,
    gk_ref,
    gv_ref,
    q_ref,
    k_ref,
    v_ref,
    g_ref,
    piece1,
    inbox1,
    zbox1,
    enter1,
    outbox1,
    state1,
    piece2,
    inbox2,
    zbox2,
    enter2,
    outbox2,
    state2,
    scores,
    mix,
    acc_k,
    acc_v,
    a_sem,
    r_sem,
    z_send,
    z_recv,
    in_sem,
    reply,
):
    J = X * C * Y
    E = Y // 2
    owners = X * C * E
    tokens = q_ref.shape[0]
    outer = lax.axis_index("outer")
    y = lax.axis_index("inner")
    c = lax.rem(outer, C)
    x = lax.rem(outer // C, X)
    z = outer // (C * X)
    me = (x * C + c) * Y + y
    OW = (0, 1, 2, 3)
    early = functools.reduce(jnp.logical_or, [y == o for o in OW])
    seat = (x * C + c) * E + jnp.clip(sum((y >= o).astype(jnp.int32) for o in OW) - 1, 0, E - 1)

    def device(zz, xx, cc, yy):
        return ((zz * X + xx) * C + cc, yy)

    def far_first(n):
        return sorted(range(1, n), key=lambda d: -min(d, n - d))

    def plane(what):
        def ring(d):
            yy = lax.rem(y + d, Y)
            for dx in far_first(X) + [0]:
                for dc in range(C):
                    if dx or dc or not isinstance(d, int):
                        xx, cc = lax.rem(x + dx, X), lax.rem(c + dc, C)
                        what((xx * C + cc) * Y + yy, device(z, xx, cc, yy))

        def far(t, _):
            ring(jnp.where(lax.rem(t, 2) == 1, Y // 2 - (t + 1) // 2, Y // 2 + t // 2))
            return 0

        lax.fori_loop(0, Y - 1, far, 0)
        ring(0)

    def to_owners(what):
        for yy in (0, 1, 2, 3):
            for dx in far_first(X) + [0]:
                for dc in range(C):
                    xx, cc = lax.rem(x + dx, X), lax.rem(c + dc, C)
                    j, p = (xx * C + cc) * E + OW.index(yy), device(z, xx, cc, yy)
                    if dx or dc:
                        what(j, p)
                    else:

                        @pl.when(y != yy)
                        def _():
                            what(j, p)

    barrier = pltpu.get_barrier_semaphore()

    @pl.when(early)
    def _():
        plane(lambda j, p: pl.semaphore_signal(barrier, inc=1, device_id=p, device_id_type=MESH))

        def greet(zz, _):
            pl.semaphore_signal(barrier, inc=1, device_id=device(zz, x, c, y), device_id_type=MESH)
            return 0

        lax.fori_loop(z + 1, Z, greet, 0)

    loads = {}
    for i, (name, src, dst) in enumerate(
        (("k", k_hbm, k_ref), ("v", v_hbm, v_ref), ("q", q_hbm, q_ref), ("g", g_hbm, g_ref))
    ):
        loads[name] = pltpu.make_async_copy(src, dst, in_sem.at[i])
        loads[name].start()

    def part(ref, h):
        return ref[:, h * DH : (h + 1) * DH]

    lower = lax.broadcasted_iota(jnp.int32, (tokens, tokens), 0) >= lax.broadcasted_iota(
        jnp.int32, (tokens, tokens), 1
    )

    def remote(src, dst, send, recv, p):
        pltpu.make_async_remote_copy(
            src_ref=src, dst_ref=dst, send_sem=send, recv_sem=recv, device_id=p, device_id_type=MESH
        ).start()

    def all_of(ref, sem):
        pltpu.make_async_copy(ref, ref, sem).wait()

    def put(piece, h, value):
        n, rows, _ = piece.shape
        piece[h * n // H : (h + 1) * n // H] = value.astype(BF16).reshape(n // H, rows, DH)

    def got(state, h):
        n = state.shape[0]
        return state[h * n // H : (h + 1) * n // H].reshape(DH, DH)

    def carry(inbox, zbox, enter, outbox, z_send, z_recv, forward):
        total = jnp.sum(inbox[...].astype(F32), axis=0)
        zbox[z] = total.astype(zbox.dtype)

        def send_z(zz, _):
            if forward:
                pl.semaphore_wait(reply.at[zz], 1)
            remote(zbox.at[z], zbox.at[z], z_send.at[zz], z_recv.at[z], device(zz, x, c, y))
            return 0

        lax.fori_loop(z + 1 if forward else 0, Z if forward else z, send_z, 0)
        run = jnp.zeros(total.shape, F32)
        for j in range(J) if forward else reversed(range(J)):
            enter[j] = run
            run = run + inbox[j].astype(F32)

        def take(i, sofar):
            all_of(zbox.at[i], z_recv.at[i])
            return sofar + zbox[i].astype(F32)

        before = lax.fori_loop(
            0 if forward else z + 1, z if forward else Z, take, jnp.zeros(total.shape, F32)
        )
        for j in range(J):
            outbox[j] = (enter[j] + before).astype(BF16)

    def drain_z(zbox, z_send, forward):
        def sent(i, _):
            all_of(zbox.at[z], z_send.at[i])
            return 0

        lax.fori_loop(z + 1 if forward else 0, Z if forward else z, sent, 0)

    loads["k"].wait()
    loads["v"].wait()
    for h in range(H):
        put(piece1, h, mm_tn(part(k_ref, h), part(v_ref, h)))
    pl.semaphore_wait(barrier, jnp.where(early, owners - 1 + z, owners))

    @pl.when(early)
    def _():
        def answer(zz, _):
            pl.semaphore_signal(
                reply.at[z], inc=1, device_id=device(zz, x, c, y), device_id_type=MESH
            )
            return 0

        lax.fori_loop(0, z, answer, 0)

    to_owners(lambda j, p: remote(piece1.at[j], inbox1.at[me], a_sem.at[0, 0], a_sem.at[0, 1], p))

    @pl.when(early)
    def _():
        inbox1[me] = piece1[seat]

    loads["q"].wait()
    loads["g"].wait()
    for h in range(H):
        raw = mm_nt(part(q_ref, h), part(k_ref, h))
        s_h = jnp.where(lower, raw, 0.0).astype(BF16)
        scores[h] = s_h
        mix[:, h * DH : (h + 1) * DH] = mm(s_h, part(v_ref, h))

    @pl.when(early)
    def _():
        all_of(inbox1.at[pl.ds(0, J - 1)], a_sem.at[0, 1])
        carry(inbox1, zbox1, enter1, outbox1, z_send.at[0], z_recv.at[0], True)
        plane(
            lambda j, p: remote(outbox1.at[j], state1.at[seat], r_sem.at[0, 0], r_sem.at[0, 1], p)
        )
        state1[seat] = outbox1[me]
        all_of(state1.at[pl.ds(0, owners - 1)], r_sem.at[0, 1])

    @pl.when(jnp.logical_not(early))
    def _():
        all_of(state1, r_sem.at[0, 1])

    grad_mixed = []
    for h in range(H):
        pref = got(state1, h)
        q = part(q_ref, h)
        mixed = part(mix, h) + mm(q, pref)
        inverse = lax.rsqrt(jnp.mean(mixed * mixed, axis=-1, keepdims=True) + eps)
        normed = mixed * inverse
        att_ref[:, h * DH : (h + 1) * DH] = normed.astype(BF16)
        g = part(g_ref, h).astype(F32)
        gm = (inverse * (g - normed * jnp.mean(g * normed, axis=-1, keepdims=True))).astype(BF16)
        grad_mixed.append(gm)
        put(piece2, h, mm_tn(q, gm))
    plane(lambda j, p: remote(piece2.at[j], inbox2.at[me], a_sem.at[1, 0], a_sem.at[1, 1], p))
    inbox2[me] = piece2[me]
    for h in range(H):
        gm = grad_mixed[h]
        gs = jnp.where(lower, mm_nt(gm, part(v_ref, h)), 0.0).astype(BF16)
        pref = got(state1, h)
        gq_ref[:, h * DH : (h + 1) * DH] = (mm(gs, part(k_ref, h)) + mm_nt(gm, pref)).astype(BF16)
        acc_k[:, h * DH : (h + 1) * DH] = mm_tn(gs, part(q_ref, h))
        acc_v[:, h * DH : (h + 1) * DH] = mm_tn(scores[h], gm)
    all_of(inbox2.at[pl.ds(0, J - 1)], a_sem.at[1, 1])
    carry(inbox2, zbox2, enter2, outbox2, z_send.at[1], z_recv.at[1], False)
    plane(lambda j, p: remote(outbox2.at[j], state2.at[me], r_sem.at[1, 0], r_sem.at[1, 1], p))
    state2[me] = outbox2[me]
    all_of(state2.at[pl.ds(0, J - 1)], r_sem.at[1, 1])
    for h in range(H):
        suf = got(state2, h)
        gk_ref[:, h * DH : (h + 1) * DH] = (part(acc_k, h) + mm_nt(part(v_ref, h), suf)).astype(BF16)
        gv_ref[:, h * DH : (h + 1) * DH] = (part(acc_v, h) + mm(part(k_ref, h), suf)).astype(BF16)

    @pl.when(early)
    def _():
        all_of(piece1.at[pl.ds(0, owners - 1)], a_sem.at[0, 0])
        drain_z(zbox1, z_send.at[0], True)
        all_of(outbox1.at[pl.ds(0, J - 1)], r_sem.at[0, 0])

    @pl.when(jnp.logical_not(early))
    def _():
        all_of(piece1, a_sem.at[0, 0])

    all_of(piece2.at[pl.ds(0, J - 1)], a_sem.at[1, 0])
    drain_z(zbox2, z_send.at[1], False)
    all_of(outbox2.at[pl.ds(0, J - 1)], r_sem.at[1, 0])


def flush(*refs):
    n = len(refs) // 2
    sem = refs[-1]
    copies = [pltpu.make_async_copy(refs[i], refs[n + i], sem.at[i]) for i in range(n)]
    for copy in copies:
        copy.start()
    for copy in copies:
        copy.wait()


def solution(mesh):
    Z = mesh.shape["outer"] // (X * C)
    Y = mesh.shape["inner"]
    J = X * C * Y
    spec = P(("outer", "inner"), None)

    def local(q, k, v, g):
        tokens, width = q.shape
        vmem = pl.BlockSpec(memory_space=pltpu.VMEM)
        def stage(owners):
            rows = (H * DH) // owners
            return [
                pltpu.VMEM((owners, rows, DH), BF16),
                pltpu.VMEM((J, rows, DH), BF16),
                pltpu.VMEM((Z, rows, DH), BF16),
                pltpu.VMEM((J, rows, DH), F32),
                pltpu.VMEM((J, rows, DH), BF16),
                pltpu.VMEM((owners, rows, DH), BF16),
            ]

        block = pltpu.VMEM((tokens, width), BF16)
        hbm = pl.BlockSpec(memory_space=pl.ANY)
        results = pl.pallas_call(
            functools.partial(kernel, Z, Y),
            out_shape=[block] * 4,
            in_specs=[hbm] * 4,
            out_specs=[vmem] * 4,
            scratch_shapes=[block] * 4
            + stage(J // 2)
            + stage(J)
            + [
                pltpu.VMEM((H, tokens, tokens), BF16),
                pltpu.VMEM((tokens, width), F32),
                pltpu.VMEM((tokens, width), F32),
                pltpu.VMEM((tokens, width), F32),
                pltpu.SemaphoreType.DMA((2, 2)),
                pltpu.SemaphoreType.DMA((2, 2)),
                pltpu.SemaphoreType.DMA((2, Z)),
                pltpu.SemaphoreType.DMA((2, Z)),
                pltpu.SemaphoreType.DMA((4,)),
                pltpu.SemaphoreType.REGULAR((Z,)),
            ],
            compiler_params=pltpu.CompilerParams(collective_id=0, has_side_effects=True),
        )(q, k, v, g)
        return pl.pallas_call(
            flush,
            out_shape=[jax.ShapeDtypeStruct((tokens, width), BF16)] * 4,
            in_specs=[vmem] * 4,
            out_specs=[hbm] * 4,
            scratch_shapes=[pltpu.SemaphoreType.DMA((4,))],
        )(*[pltpu.with_memory_space_constraint(r, pltpu.VMEM) for r in results])

    return jax.shard_map(
        local, mesh=mesh, in_specs=(spec,) * 4, out_specs=(spec,) * 4, check_vma=False
    )
```

```python
import functools

import jax
import jax.numpy as jnp
from jax import lax
from jax.experimental import pallas as pl
from jax.experimental.pallas import tpu as pltpu
from jax.sharding import PartitionSpec as P

H = 2
DH = 128
X = 4
C = 2
eps = 1e-06
MESH = pl.DeviceIdType.MESH
F32 = jnp.float32
BF16 = jnp.bfloat16


def mm(a, b):
    return lax.dot_general(a, b, (((1,), (0,)), ((), ())), preferred_element_type=F32)


def mm_nt(a, b):
    return lax.dot_general(a, b, (((1,), (1,)), ((), ())), preferred_element_type=F32)


def mm_tn(a, b):
    return lax.dot_general(a, b, (((0,), (0,)), ((), ())), preferred_element_type=F32)


def kernel(
    Z,
    Y,
    q_hbm,
    k_hbm,
    v_hbm,
    g_hbm,
    att_ref,
    gq_ref,
    gk_ref,
    gv_ref,
    q_ref,
    k_ref,
    v_ref,
    g_ref,
    piece1,
    inbox1,
    zbox1,
    enter1,
    outbox1,
    state1,
    piece2,
    inbox2,
    zbox2,
    enter2,
    outbox2,
    state2,
    scores,
    mix,
    acc_k,
    acc_v,
    a_sem,
    r_sem,
    z_send,
    z_recv,
    in_sem,
    reply,
):
    J = X * C * Y
    E = Y // 2
    owners = X * C * E
    tokens = q_ref.shape[0]
    outer = lax.axis_index("outer")
    y = lax.axis_index("inner")
    c = lax.rem(outer, C)
    x = lax.rem(outer // C, X)
    z = outer // (C * X)
    me = (x * C + c) * Y + y
    OW = (0, 1, 2, 3)
    early = functools.reduce(jnp.logical_or, [y == o for o in OW])
    seat = (x * C + c) * E + jnp.clip(sum((y >= o).astype(jnp.int32) for o in OW) - 1, 0, E - 1)

    def device(zz, xx, cc, yy):
        return ((zz * X + xx) * C + cc, yy)

    def far_first(n):
        return sorted(range(1, n), key=lambda d: -min(d, n - d))

    def plane(what):
        def ring(d):
            yy = lax.rem(y + d, Y)
            for dx in far_first(X) + [0]:
                for dc in range(C):
                    if dx or dc or not isinstance(d, int):
                        xx, cc = lax.rem(x + dx, X), lax.rem(c + dc, C)
                        what((xx * C + cc) * Y + yy, device(z, xx, cc, yy))

        def far(t, _):
            ring(jnp.where(lax.rem(t, 2) == 1, Y // 2 - (t + 1) // 2, Y // 2 + t // 2))
            return 0

        lax.fori_loop(0, Y - 1, far, 0)
        ring(0)

    def to_owners(what):
        for yy in (0, 1, 2, 3):
            for dx in far_first(X) + [0]:
                for dc in range(C):
                    xx, cc = lax.rem(x + dx, X), lax.rem(c + dc, C)
                    j, p = (xx * C + cc) * E + OW.index(yy), device(z, xx, cc, yy)
                    if dx or dc:
                        what(j, p)
                    else:

                        @pl.when(y != yy)
                        def _():
                            what(j, p)

    barrier = pltpu.get_barrier_semaphore()

    @pl.when(early)
    def _():
        plane(lambda j, p: pl.semaphore_signal(barrier, inc=1, device_id=p, device_id_type=MESH))

        def greet(zz, _):
            pl.semaphore_signal(barrier, inc=1, device_id=device(zz, x, c, y), device_id_type=MESH)
            return 0

        lax.fori_loop(z + 1, Z, greet, 0)

    loads = {}
    for i, (name, src, dst) in enumerate(
        (("k", k_hbm, k_ref), ("v", v_hbm, v_ref), ("q", q_hbm, q_ref), ("g", g_hbm, g_ref))
    ):
        loads[name] = pltpu.make_async_copy(src, dst, in_sem.at[i])
        step = src.shape[0] // 4
        for t in range(4):
            pltpu.make_async_copy(
                src.at[pl.ds(t * step, step)], dst.at[pl.ds(t * step, step)], in_sem.at[i]
            ).start()

    def part(ref, h):
        return ref[:, h * DH : (h + 1) * DH]

    lower = lax.broadcasted_iota(jnp.int32, (tokens, tokens), 0) >= lax.broadcasted_iota(
        jnp.int32, (tokens, tokens), 1
    )

    def remote(src, dst, send, recv, p):
        pltpu.make_async_remote_copy(
            src_ref=src, dst_ref=dst, send_sem=send, recv_sem=recv, device_id=p, device_id_type=MESH
        ).start()

    def all_of(ref, sem):
        pltpu.make_async_copy(ref, ref, sem).wait()

    def put(piece, h, value):
        n, rows, _ = piece.shape
        piece[h * n // H : (h + 1) * n // H] = value.astype(BF16).reshape(n // H, rows, DH)

    def got(state, h):
        n = state.shape[0]
        return state[h * n // H : (h + 1) * n // H].reshape(DH, DH)

    def carry(inbox, zbox, enter, outbox, z_send, z_recv, forward):
        total = jnp.sum(inbox[...].astype(F32), axis=0)
        zbox[z] = total.astype(zbox.dtype)

        def send_z(zz, _):
            remote(zbox.at[z], zbox.at[z], z_send.at[zz], z_recv.at[z], device(zz, x, c, y))
            return 0

        if forward:

            @pl.when(z < Z - 1)
            def _():
                pl.semaphore_wait(reply, Z - 1 - z)

        lax.fori_loop(z + 1 if forward else 0, Z if forward else z, send_z, 0)
        run = jnp.zeros(total.shape, F32)
        for j in range(J) if forward else reversed(range(J)):
            enter[j] = run
            run = run + inbox[j].astype(F32)

        def take(i, sofar):
            all_of(zbox.at[i], z_recv.at[i])
            return sofar + zbox[i].astype(F32)

        before = lax.fori_loop(
            0 if forward else z + 1, z if forward else Z, take, jnp.zeros(total.shape, F32)
        )
        for j in range(J):
            outbox[j] = (enter[j] + before).astype(BF16)

    def drain_z(zbox, z_send, forward):
        def sent(i, _):
            all_of(zbox.at[z], z_send.at[i])
            return 0

        lax.fori_loop(z + 1 if forward else 0, Z if forward else z, sent, 0)

    loads["k"].wait()
    loads["v"].wait()
    for h in range(H):
        put(piece1, h, mm_tn(part(k_ref, h), part(v_ref, h)))
    pl.semaphore_wait(barrier, jnp.where(early, owners - 1 + z, owners))

    @pl.when(early)
    def _():
        def answer(zz, _):
            pl.semaphore_signal(
                reply, inc=1, device_id=device(zz, x, c, y), device_id_type=MESH
            )
            return 0

        lax.fori_loop(0, z, answer, 0)

    to_owners(lambda j, p: remote(piece1.at[j], inbox1.at[me], a_sem.at[0, 0], a_sem.at[0, 1], p))

    @pl.when(early)
    def _():
        inbox1[me] = piece1[seat]

    loads["q"].wait()
    loads["g"].wait()
    for h in range(H):
        raw = mm_nt(part(q_ref, h), part(k_ref, h))
        s_h = jnp.where(lower, raw, 0.0).astype(BF16)
        scores[h] = s_h
        mix[:, h * DH : (h + 1) * DH] = mm(s_h, part(v_ref, h))

    @pl.when(early)
    def _():
        all_of(inbox1.at[pl.ds(0, J - 1)], a_sem.at[0, 1])
        carry(inbox1, zbox1, enter1, outbox1, z_send.at[0], z_recv.at[0], True)
        plane(
            lambda j, p: remote(outbox1.at[j], state1.at[seat], r_sem.at[0, 0], r_sem.at[0, 1], p)
        )
        state1[seat] = outbox1[me]
        all_of(state1.at[pl.ds(0, owners - 1)], r_sem.at[0, 1])

    @pl.when(jnp.logical_not(early))
    def _():
        all_of(state1, r_sem.at[0, 1])

    grad_mixed = []
    for h in range(H):
        pref = got(state1, h)
        q = part(q_ref, h)
        mixed = part(mix, h) + mm(q, pref)
        inverse = lax.rsqrt(jnp.mean(mixed * mixed, axis=-1, keepdims=True) + eps)
        normed = mixed * inverse
        att_ref[:, h * DH : (h + 1) * DH] = normed.astype(BF16)
        g = part(g_ref, h).astype(F32)
        gm = (inverse * (g - normed * jnp.mean(g * normed, axis=-1, keepdims=True))).astype(BF16)
        grad_mixed.append(gm)
        put(piece2, h, mm_tn(q, gm))
    plane(lambda j, p: remote(piece2.at[j], inbox2.at[me], a_sem.at[1, 0], a_sem.at[1, 1], p))
    inbox2[me] = piece2[me]
    for h in range(H):
        gm = grad_mixed[h]
        gs = jnp.where(lower, mm_nt(gm, part(v_ref, h)), 0.0).astype(BF16)
        pref = got(state1, h)
        gq_ref[:, h * DH : (h + 1) * DH] = (mm(gs, part(k_ref, h)) + mm_nt(gm, pref)).astype(BF16)
        acc_k[:, h * DH : (h + 1) * DH] = mm_tn(gs, part(q_ref, h))
        acc_v[:, h * DH : (h + 1) * DH] = mm_tn(scores[h], gm)
    all_of(inbox2.at[pl.ds(0, J - 1)], a_sem.at[1, 1])
    carry(inbox2, zbox2, enter2, outbox2, z_send.at[1], z_recv.at[1], False)
    plane(lambda j, p: remote(outbox2.at[j], state2.at[me], r_sem.at[1, 0], r_sem.at[1, 1], p))
    state2[me] = outbox2[me]
    all_of(state2.at[pl.ds(0, J - 1)], r_sem.at[1, 1])
    for h in range(H):
        suf = got(state2, h)
        gk_ref[:, h * DH : (h + 1) * DH] = (part(acc_k, h) + mm_nt(part(v_ref, h), suf)).astype(BF16)
        gv_ref[:, h * DH : (h + 1) * DH] = (part(acc_v, h) + mm(part(k_ref, h), suf)).astype(BF16)

    @pl.when(early)
    def _():
        all_of(piece1.at[pl.ds(0, owners - 1)], a_sem.at[0, 0])
        drain_z(zbox1, z_send.at[0], True)
        all_of(outbox1.at[pl.ds(0, J - 1)], r_sem.at[0, 0])

    @pl.when(jnp.logical_not(early))
    def _():
        all_of(piece1, a_sem.at[0, 0])

    all_of(piece2.at[pl.ds(0, J - 1)], a_sem.at[1, 0])
    drain_z(zbox2, z_send.at[1], False)
    all_of(outbox2.at[pl.ds(0, J - 1)], r_sem.at[1, 0])


def flush(*refs):
    n = len(refs) // 2
    sem = refs[-1]
    copies = [pltpu.make_async_copy(refs[i], refs[n + i], sem.at[i]) for i in range(n)]
    for copy in copies:
        copy.start()
    for copy in copies:
        copy.wait()


def solution(mesh):
    Z = mesh.shape["outer"] // (X * C)
    Y = mesh.shape["inner"]
    J = X * C * Y
    spec = P(("outer", "inner"), None)

    def local(q, k, v, g):
        tokens, width = q.shape
        vmem = pl.BlockSpec(memory_space=pltpu.VMEM)
        def stage(owners):
            rows = (H * DH) // owners
            return [
                pltpu.VMEM((owners, rows, DH), BF16),
                pltpu.VMEM((J, rows, DH), BF16),
                pltpu.VMEM((Z, rows, DH), BF16),
                pltpu.VMEM((J, rows, DH), F32),
                pltpu.VMEM((J, rows, DH), BF16),
                pltpu.VMEM((owners, rows, DH), BF16),
            ]

        block = pltpu.VMEM((tokens, width), BF16)
        hbm = pl.BlockSpec(memory_space=pl.ANY)
        results = pl.pallas_call(
            functools.partial(kernel, Z, Y),
            out_shape=[block] * 4,
            in_specs=[hbm] * 4,
            out_specs=[vmem] * 4,
            scratch_shapes=[block] * 4
            + stage(J // 2)
            + stage(J)
            + [
                pltpu.VMEM((H, tokens, tokens), BF16),
                pltpu.VMEM((tokens, width), F32),
                pltpu.VMEM((tokens, width), F32),
                pltpu.VMEM((tokens, width), F32),
                pltpu.SemaphoreType.DMA((2, 2)),
                pltpu.SemaphoreType.DMA((2, 2)),
                pltpu.SemaphoreType.DMA((2, Z)),
                pltpu.SemaphoreType.DMA((2, Z)),
                pltpu.SemaphoreType.DMA((4,)),
                pltpu.SemaphoreType.REGULAR,
            ],
            compiler_params=pltpu.CompilerParams(collective_id=0, has_side_effects=True),
        )(q, k, v, g)
        return pl.pallas_call(
            flush,
            out_shape=[jax.ShapeDtypeStruct((tokens, width), BF16)] * 4,
            in_specs=[vmem] * 4,
            out_specs=[hbm] * 4,
            scratch_shapes=[pltpu.SemaphoreType.DMA((4,))],
        )(*[pltpu.with_memory_space_constraint(r, pltpu.VMEM) for r in results])

    return jax.shard_map(
        local, mesh=mesh, in_specs=(spec,) * 4, out_specs=(spec,) * 4, check_vma=False
    )
```

```python
import functools

import jax
import jax.numpy as jnp
from jax import lax
from jax.experimental import pallas as pl
from jax.experimental.pallas import tpu as pltpu
from jax.sharding import PartitionSpec as P

H = 2
DH = 128
X = 4
C = 2
eps = 1e-06
MESH = pl.DeviceIdType.MESH
F32 = jnp.float32
BF16 = jnp.bfloat16


def mm(a, b):
    return lax.dot_general(a, b, (((1,), (0,)), ((), ())), preferred_element_type=F32)


def mm_nt(a, b):
    return lax.dot_general(a, b, (((1,), (1,)), ((), ())), preferred_element_type=F32)


def mm_tn(a, b):
    return lax.dot_general(a, b, (((0,), (0,)), ((), ())), preferred_element_type=F32)


def kernel(
    Z,
    Y,
    q_hbm,
    k_hbm,
    v_hbm,
    g_hbm,
    att_ref,
    gq_ref,
    gk_ref,
    gv_ref,
    q_ref,
    k_ref,
    v_ref,
    g_ref,
    piece1,
    inbox1,
    zbox1,
    enter1,
    outbox1,
    state1,
    piece2,
    inbox2,
    zbox2,
    enter2,
    outbox2,
    state2,
    flipped,
    scores,
    mix,
    acc_k,
    acc_v,
    a_sem,
    r_sem,
    z_send,
    z_recv,
    in_sem,
    reply,
):
    J = X * C * Y
    E = Y // 2
    owners = X * C * E
    tokens = q_ref.shape[0]
    outer = lax.axis_index("outer")
    y = lax.axis_index("inner")
    c = lax.rem(outer, C)
    x = lax.rem(outer // C, X)
    z = outer // (C * X)
    me = (x * C + c) * Y + y
    OW = (0, 1, 2, 3)
    early = functools.reduce(jnp.logical_or, [y == o for o in OW])
    seat = (x * C + c) * E + jnp.clip(sum((y >= o).astype(jnp.int32) for o in OW) - 1, 0, E - 1)

    def device(zz, xx, cc, yy):
        return ((zz * X + xx) * C + cc, yy)

    def far_first(n):
        return sorted(range(1, n), key=lambda d: -min(d, n - d))

    def plane(what):
        def ring(d):
            yy = lax.rem(y + d, Y)
            for dx in far_first(X) + [0]:
                for dc in range(C):
                    if dx or dc or not isinstance(d, int):
                        xx, cc = lax.rem(x + dx, X), lax.rem(c + dc, C)
                        what((xx * C + cc) * Y + yy, device(z, xx, cc, yy))

        def far(t, _):
            ring(jnp.where(lax.rem(t, 2) == 1, Y // 2 - (t + 1) // 2, Y // 2 + t // 2))
            return 0

        lax.fori_loop(0, Y - 1, far, 0)
        ring(0)

    def to_owners(what):
        for yy in (0, 1, 2, 3):
            for dx in far_first(X) + [0]:
                for dc in range(C):
                    xx, cc = lax.rem(x + dx, X), lax.rem(c + dc, C)
                    j, p = (xx * C + cc) * E + OW.index(yy), device(z, xx, cc, yy)
                    if dx or dc:
                        what(j, p)
                    else:

                        @pl.when(y != yy)
                        def _():
                            what(j, p)

    barrier = pltpu.get_barrier_semaphore()

    @pl.when(early)
    def _():
        plane(lambda j, p: pl.semaphore_signal(barrier, inc=1, device_id=p, device_id_type=MESH))

        def greet(zz, _):
            pl.semaphore_signal(barrier, inc=1, device_id=device(zz, x, c, y), device_id_type=MESH)
            return 0

        lax.fori_loop(z + 1, Z, greet, 0)

    loads = {}
    for i, (name, src, dst) in enumerate(
        (("k", k_hbm, k_ref), ("v", v_hbm, v_ref), ("q", q_hbm, q_ref), ("g", g_hbm, g_ref))
    ):
        loads[name] = pltpu.make_async_copy(src, dst, in_sem.at[i])
        step = src.shape[0] // 4
        for t in range(4):
            pltpu.make_async_copy(
                src.at[pl.ds(t * step, step)], dst.at[pl.ds(t * step, step)], in_sem.at[i]
            ).start()

    def part(ref, h):
        return ref[:, h * DH : (h + 1) * DH]

    lower = lax.broadcasted_iota(jnp.int32, (tokens, tokens), 0) >= lax.broadcasted_iota(
        jnp.int32, (tokens, tokens), 1
    )

    def remote(src, dst, send, recv, p):
        pltpu.make_async_remote_copy(
            src_ref=src, dst_ref=dst, send_sem=send, recv_sem=recv, device_id=p, device_id_type=MESH
        ).start()

    def all_of(ref, sem):
        pltpu.make_async_copy(ref, ref, sem).wait()

    def put(piece, h, value):
        n, rows, _ = piece.shape
        piece[h * n // H : (h + 1) * n // H] = value.astype(BF16).reshape(n // H, rows, DH)

    def got(state, h):
        n = state.shape[0]
        return state[h * n // H : (h + 1) * n // H].reshape(DH, DH)

    def carry(inbox, zbox, enter, outbox, z_send, z_recv, forward):
        total = jnp.sum(inbox[...].astype(F32), axis=0)
        zbox[z] = total.astype(zbox.dtype)

        def send_z(zz, _):
            remote(zbox.at[z], zbox.at[z], z_send.at[zz], z_recv.at[z], device(zz, x, c, y))
            return 0

        if forward:

            @pl.when(z < Z - 1)
            def _():
                pl.semaphore_wait(reply, Z - 1 - z)

        lax.fori_loop(z + 1 if forward else 0, Z if forward else z, send_z, 0)
        run = jnp.zeros(total.shape, F32)
        for j in range(J) if forward else reversed(range(J)):
            enter[j] = run
            run = run + inbox[j].astype(F32)

        def take(i, sofar):
            all_of(zbox.at[i], z_recv.at[i])
            return sofar + zbox[i].astype(F32)

        before = lax.fori_loop(
            0 if forward else z + 1, z if forward else Z, take, jnp.zeros(total.shape, F32)
        )
        for j in range(J):
            outbox[j] = (enter[j] + before).astype(BF16)

    def drain_z(zbox, z_send, forward):
        def sent(i, _):
            all_of(zbox.at[z], z_send.at[i])
            return 0

        lax.fori_loop(z + 1 if forward else 0, Z if forward else z, sent, 0)

    loads["k"].wait()
    loads["v"].wait()
    for h in range(H):
        put(piece1, h, mm_tn(part(k_ref, h), part(v_ref, h)))
    pl.semaphore_wait(barrier, jnp.where(early, owners - 1 + z, owners))

    @pl.when(early)
    def _():
        def answer(zz, _):
            pl.semaphore_signal(
                reply, inc=1, device_id=device(zz, x, c, y), device_id_type=MESH
            )
            return 0

        lax.fori_loop(0, z, answer, 0)

    to_owners(lambda j, p: remote(piece1.at[j], inbox1.at[me], a_sem.at[0, 0], a_sem.at[0, 1], p))

    @pl.when(early)
    def _():
        inbox1[me] = piece1[seat]

    loads["q"].wait()
    loads["g"].wait()
    for h in range(H):
        raw = mm_nt(part(q_ref, h), part(k_ref, h))
        s_h = jnp.where(lower, raw, 0.0).astype(BF16)
        scores[h] = s_h
        flipped[h * DH : (h + 1) * DH] = part(q_ref, h).T
        mix[:, h * DH : (h + 1) * DH] = mm(s_h, part(v_ref, h))

    @pl.when(early)
    def _():
        all_of(inbox1.at[pl.ds(0, J - 1)], a_sem.at[0, 1])
        carry(inbox1, zbox1, enter1, outbox1, z_send.at[0], z_recv.at[0], True)
        plane(
            lambda j, p: remote(outbox1.at[j], state1.at[seat], r_sem.at[0, 0], r_sem.at[0, 1], p)
        )
        state1[seat] = outbox1[me]
        all_of(state1.at[pl.ds(0, owners - 1)], r_sem.at[0, 1])

    @pl.when(jnp.logical_not(early))
    def _():
        all_of(state1, r_sem.at[0, 1])

    grad_mixed = []
    for h in range(H):
        pref = got(state1, h)
        q = part(q_ref, h)
        mixed = part(mix, h) + mm(q, pref)
        inverse = lax.rsqrt(jnp.mean(mixed * mixed, axis=-1, keepdims=True) + eps)
        normed = mixed * inverse
        att_ref[:, h * DH : (h + 1) * DH] = normed.astype(BF16)
        g = part(g_ref, h).astype(F32)
        gm = (inverse * (g - normed * jnp.mean(g * normed, axis=-1, keepdims=True))).astype(BF16)
        grad_mixed.append(gm)
        put(piece2, h, mm(flipped[h * DH : (h + 1) * DH], gm))
    plane(lambda j, p: remote(piece2.at[j], inbox2.at[me], a_sem.at[1, 0], a_sem.at[1, 1], p))
    inbox2[me] = piece2[me]
    for h in range(H):
        gm = grad_mixed[h]
        gs = jnp.where(lower, mm_nt(gm, part(v_ref, h)), 0.0).astype(BF16)
        pref = got(state1, h)
        gq_ref[:, h * DH : (h + 1) * DH] = (mm(gs, part(k_ref, h)) + mm_nt(gm, pref)).astype(BF16)
        acc_k[:, h * DH : (h + 1) * DH] = mm_tn(gs, part(q_ref, h))
        acc_v[:, h * DH : (h + 1) * DH] = mm_tn(scores[h], gm)
    all_of(inbox2.at[pl.ds(0, J - 1)], a_sem.at[1, 1])
    carry(inbox2, zbox2, enter2, outbox2, z_send.at[1], z_recv.at[1], False)
    plane(lambda j, p: remote(outbox2.at[j], state2.at[me], r_sem.at[1, 0], r_sem.at[1, 1], p))
    state2[me] = outbox2[me]
    all_of(state2.at[pl.ds(0, J - 1)], r_sem.at[1, 1])
    for h in range(H):
        suf = got(state2, h)
        gk_ref[:, h * DH : (h + 1) * DH] = (part(acc_k, h) + mm_nt(part(v_ref, h), suf)).astype(BF16)
        gv_ref[:, h * DH : (h + 1) * DH] = (part(acc_v, h) + mm(part(k_ref, h), suf)).astype(BF16)

    @pl.when(early)
    def _():
        all_of(piece1.at[pl.ds(0, owners - 1)], a_sem.at[0, 0])
        drain_z(zbox1, z_send.at[0], True)
        all_of(outbox1.at[pl.ds(0, J - 1)], r_sem.at[0, 0])

    @pl.when(jnp.logical_not(early))
    def _():
        all_of(piece1, a_sem.at[0, 0])

    all_of(piece2.at[pl.ds(0, J - 1)], a_sem.at[1, 0])
    drain_z(zbox2, z_send.at[1], False)
    all_of(outbox2.at[pl.ds(0, J - 1)], r_sem.at[1, 0])


def flush(*refs):
    n = len(refs) // 2
    sem = refs[-1]
    copies = [pltpu.make_async_copy(refs[i], refs[n + i], sem.at[i]) for i in range(n)]
    for copy in copies:
        copy.start()
    for copy in copies:
        copy.wait()


def solution(mesh):
    Z = mesh.shape["outer"] // (X * C)
    Y = mesh.shape["inner"]
    J = X * C * Y
    spec = P(("outer", "inner"), None)

    def local(q, k, v, g):
        tokens, width = q.shape
        vmem = pl.BlockSpec(memory_space=pltpu.VMEM)
        def stage(owners):
            rows = (H * DH) // owners
            return [
                pltpu.VMEM((owners, rows, DH), BF16),
                pltpu.VMEM((J, rows, DH), BF16),
                pltpu.VMEM((Z, rows, DH), BF16),
                pltpu.VMEM((J, rows, DH), F32),
                pltpu.VMEM((J, rows, DH), BF16),
                pltpu.VMEM((owners, rows, DH), BF16),
            ]

        block = pltpu.VMEM((tokens, width), BF16)
        hbm = pl.BlockSpec(memory_space=pl.ANY)
        results = pl.pallas_call(
            functools.partial(kernel, Z, Y),
            out_shape=[block] * 4,
            in_specs=[hbm] * 4,
            out_specs=[vmem] * 4,
            scratch_shapes=[block] * 4
            + stage(J // 2)
            + stage(J)
            + [
                pltpu.VMEM((width, tokens), BF16),
                pltpu.VMEM((H, tokens, tokens), BF16),
                pltpu.VMEM((tokens, width), F32),
                pltpu.VMEM((tokens, width), F32),
                pltpu.VMEM((tokens, width), F32),
                pltpu.SemaphoreType.DMA((2, 2)),
                pltpu.SemaphoreType.DMA((2, 2)),
                pltpu.SemaphoreType.DMA((2, Z)),
                pltpu.SemaphoreType.DMA((2, Z)),
                pltpu.SemaphoreType.DMA((4,)),
                pltpu.SemaphoreType.REGULAR,
            ],
            compiler_params=pltpu.CompilerParams(collective_id=0, has_side_effects=True),
        )(q, k, v, g)
        return pl.pallas_call(
            flush,
            out_shape=[jax.ShapeDtypeStruct((tokens, width), BF16)] * 4,
            in_specs=[vmem] * 4,
            out_specs=[hbm] * 4,
            scratch_shapes=[pltpu.SemaphoreType.DMA((4,))],
        )(*[pltpu.with_memory_space_constraint(r, pltpu.VMEM) for r in results])

    return jax.shard_map(
        local, mesh=mesh, in_specs=(spec,) * 4, out_specs=(spec,) * 4, check_vma=False
    )
```
